32 devices in a mesh: rows: 8 (over z, y), rhs: 4 (over x, core).
Axes of the slice: x: 2, y: 2, z: 4, core: 2. Of those that a mesh axis runs over, the one named last changes fastest.
Arguments:
- right_sides: bfloat16 [64, 16384], P('rhs', 'rows'), may hold values from -6 to 6
- lower_inverse: bfloat16 [64, 256, 256], P('rows'), may hold values from -0.375 to 0.375
- lower_left: bfloat16 [64, 256, 32], P('rows'), may hold values from -1 to 1
- lower_right: bfloat16 [64, 256, 32], P('rows'), may hold values from -0.015625 to 0.015625
- upper_inverse: bfloat16 [64, 256, 256], P('rows'), may hold values from -0.375 to 0.375
- upper_left: bfloat16 [64, 256, 32], P('rows'), may hold values from -1 to 1
- upper_right: bfloat16 [64, 256, 32], P('rows'), may hold values from -0.015625 to 0.015625
- block_ranks: int32 [2, 64], P(None, 'rows'), may hold values from 8 to 32
Outputs:
- first_solve: float32 [64, 16384], P('rhs', 'rows')
- second_solve: float32 [64, 16384], P('rhs', 'rows')
The draws below stay inside these ranges and needn't reach their ends.
All inputs are finite; a program needn't handle non-finite values.
Results may differ from the reference program's by a relative error of at most 0.0051.
Values may be sent and summed in bfloat16 or wider, within the bound.
A program may use at most 64 MiB of HBM per device.

```python
import jax
import jax.numpy as jnp
from jax import lax

BS = 256
RANK = 32
RHS = 64
NBLK = 64
ORDER = 16384


def with_ends(drawn, own_key, low, largest):
    place = [jax.random.randint(jax.random.fold_in(own_key, axis), (), 0, length) for axis, length in enumerate(drawn.shape)]
    main_axis = drawn.shape.index(max(drawn.shape))
    beside = place[:main_axis] + [(place[main_axis] + 1) % drawn.shape[main_axis]] + place[main_axis + 1:]
    return drawn.at[tuple(place)].set(low).at[tuple(beside)].set(largest)


def levels(rng, extent, shards, least, high):
    gain = 1.0
    for position, shards_of in shards:
        heights = jax.random.uniform(jax.random.fold_in(jax.random.fold_in(rng, 6), position), (shards_of,), jnp.float32, least / len(shards), high / len(shards))
        gain = gain * jnp.repeat(jnp.exp(heights), extent[position] // shards_of).reshape((-1,) + (1,) * (len(extent) - 1 - position))
    return gain


def bell_draw(own_key, shape, deviation, bound, pieces=(), kind=jnp.bfloat16):
    entries = jax.random.normal(own_key, shape, jnp.float32) * deviation
    if len(pieces) > 0:
        entries = levels(own_key, shape, pieces, -0.22, 0.18) * entries
    return jnp.clip(entries, min=-bound, max=bound).astype(kind)


def setup_inputs(seed: int = 0) -> dict:
    arg_keys = jax.random.split(jax.random.key(seed), 9)
    right_sides = bell_draw(arg_keys[0], (RHS, ORDER), 1.0, 6.0, ((0, 4), (1, 8)))
    lower_inverse = bell_draw(arg_keys[1], (NBLK, BS, BS), BS ** -0.5, 0.375, ((0, 8),))
    lower_left = bell_draw(arg_keys[2], (NBLK, BS, RANK), RANK ** -0.5, 1.0, ((0, 8),))
    lower_right = bell_draw(arg_keys[3], (NBLK, BS, RANK), (8 * NBLK * BS) ** -0.5, 0.015625, ((0, 8),))
    upper_inverse = bell_draw(arg_keys[4], (NBLK, BS, BS), BS ** -0.5, 0.375, ((0, 8),))
    upper_left = bell_draw(arg_keys[5], (NBLK, BS, RANK), RANK ** -0.5, 1.0, ((0, 8),))
    upper_right = bell_draw(arg_keys[6], (NBLK, BS, RANK), (8 * NBLK * BS) ** -0.5, 0.015625, ((0, 8),))
    block_ranks = with_ends(jax.random.randint(arg_keys[7], (2, NBLK), RANK // 4, RANK + 1), jax.random.fold_in(arg_keys[7], 1), RANK // 4, RANK).astype(jnp.int32)
    return {"right_sides": right_sides, "lower_inverse": lower_inverse, "lower_left": lower_left, "lower_right": lower_right, "upper_inverse": upper_inverse, "upper_left": upper_left, "upper_right": upper_right, "block_ranks": block_ranks}


highest = lax.Precision.HIGHEST


def factors(inverse, left_factor, right_factor, ranks_row):
    product = jnp.einsum("bij,bjk->bik", inverse.astype(jnp.float32), left_factor.astype(jnp.float32))
    rounded = lax.optimization_barrier(product.astype(jnp.bfloat16))
    coupled = rounded.astype(jnp.float32)
    columns = jnp.arange(RANK, dtype=jnp.int32)
    rank_mask = (columns[None, :] < ranks_row[:, None]).astype(jnp.float32)
    masked = right_factor.astype(jnp.float32) * rank_mask[:, None, :]
    return coupled, masked


def sweep_blocks(values, inverse, coupled, masked, reverse):
    blocked = values.reshape(RHS, NBLK, BS).astype(jnp.float32)
    pushed = jnp.einsum("rbk,bjk->brj", blocked, inverse.astype(jnp.float32))

    def advance(state, inputs):
        pushed_row, coupled_row, masked_row = inputs
        solved = pushed_row - jnp.dot(state, coupled_row.T, precision=highest)
        state = state + jnp.dot(solved, masked_row, precision=highest)
        return state, solved

    start = jnp.zeros((RHS, RANK), jnp.float32)
    _, solved = lax.scan(advance, start, (pushed, coupled, masked), reverse=reverse)
    return jnp.transpose(solved, (1, 0, 2)).reshape(RHS, NBLK * BS)


def reference(right_sides, lower_inverse, lower_left, lower_right, upper_inverse, upper_left, upper_right, block_ranks):
    lower_coupled, lower_masked = factors(lower_inverse, lower_left, lower_right, block_ranks[0])
    upper_coupled, upper_masked = factors(upper_inverse, upper_left, upper_right, block_ranks[1])
    forward = sweep_blocks(right_sides, lower_inverse, lower_coupled, lower_masked, False)
    first_solve = sweep_blocks(forward.astype(jnp.bfloat16), upper_inverse, upper_coupled, upper_masked, True)
    forward_again = sweep_blocks(first_solve.astype(jnp.bfloat16), lower_inverse, lower_coupled, lower_masked, False)
    second_solve = sweep_blocks(forward_again.astype(jnp.bfloat16), upper_inverse, upper_coupled, upper_masked, True)
    return first_solve, second_solve
```

```python
import functools

import jax
import jax.numpy as jnp
from jax import lax
from jax.experimental import pallas as pl
from jax.experimental.pallas import tpu as pltpu
from jax.sharding import PartitionSpec as P

MESH = pl.DeviceIdType.MESH
LANES = 128
f32, bf16 = jnp.float32, jnp.bfloat16


def split(x):
    hi = x.astype(bf16)
    return hi, (x - hi.astype(f32)).astype(bf16)


def dot(a, b):
    return jnp.dot(a, b, preferred_element_type=f32)


def dot_nt(a, b):
    return lax.dot_general(a, b, (((1,), (1,)), ((), ())), preferred_element_type=f32)


def dot_split(a, b_hi, b_lo):
    a_hi, a_lo = split(a)
    rows = a.shape[0]
    both = dot(jnp.concatenate([a_hi, a_lo], axis=0), b_hi)
    return both[:rows] + both[rows:] + dot(a_hi, b_lo)


def dot_full(a, b):
    return dot_split(a, *split(b))


def each(count, body):
    if count <= 8:
        for i in range(count):
            body(i)
    else:
        lax.fori_loop(0, count, lambda i, c: (body(i), c)[1], 0)


def kernel(
    R, nb, bs, w, n,
    rhs, linv_h, llt, lrt, uinv_h, ult, urt, ranks,
    first, second,
    inv, ctp, ntp, wst, hs, got1, got2, send1, send2, g, table, y,
    load_sem, send_sem, recv_sem,
):
    me = lax.axis_index("rows")
    group = LANES // w
    quads = nb // group
    half = n // 2

    loads = []
    for f, src in ((0, linv_h), (1, uinv_h)):
        cp = pltpu.make_async_copy(src, inv.at[f], load_sem.at[f])
        cp.start()
        loads.append(cp)

    barrier = pltpu.get_barrier_semaphore()

    def greet(i):
        pl.semaphore_signal(
            barrier, inc=1, device_id={"rows": lax.rem(me + i + 1, R)}, device_id_type=MESH
        )

    each(R - 1, greet)

    ctp[...] = jnp.zeros_like(ctp)
    ntp[...] = jnp.zeros_like(ntp)

    lane = lax.broadcasted_iota(jnp.int32, (w, LANES), 1)
    row = lax.broadcasted_iota(jnp.int32, (w, LANES), 0)
    eye = (lax.rem(lane, w) == row).astype(f32)

    def lanes(rows):
        return lax.broadcasted_iota(jnp.int32, (rows, LANES), 1)

    def block(f, p):
        return p if f == 0 else nb - 1 - p

    lefts, rights = (llt, ult), (lrt, urt)
    kernels = ([], [])
    maps = [None, None]
    for f in (0, 1):
        loads[f].wait()
        wide_row = lax.broadcasted_iota(jnp.int32, (w, bs), 0)
        for p in range(nb):
            b = block(f, p)
            at = pl.ds(w * (p % group), w)
            ct = dot_nt(lefts[f][b], inv[f, b]).astype(bf16)
            ctp[f, p, at, :] = ct
            mt = jnp.where(wide_row < ranks[f, b], rights[f][b].astype(f32), 0.0).astype(bf16)
            hi, lo = split(dot(mt, inv[f, b]))
            ntp[f, 0, p, at, :] = hi
            ntp[f, 1, p, at, :] = lo
            kernels[f].append(eye - dot_nt(ct, jnp.concatenate([mt] * group, axis=0)))

    running = [eye, eye]
    columns = ([], [])
    for p in range(nb):
        for f in (0, 1):
            columns[f].append(running[f])
            moved = dot_full(running[f][:, :w], kernels[f][p])
            running[f] = jnp.concatenate([moved, eye], axis=0)

    full = w * (nb + 1)
    for f in (0, 1):
        maps[f] = running[f][:w]
        hi, lo = split(running[f][w:])
        wst[f, 0, quads] = hi
        wst[f, 1, quads] = lo
        for q in range(quads):
            total = jnp.zeros((full, LANES), f32)
            for k in range(group):
                col = columns[f][q * group + k]
                grown = jnp.concatenate([col, jnp.zeros((full - col.shape[0], LANES), f32)], axis=0)
                total = jnp.where(lanes(full) // w == k, grown, total)
            hi, lo = split(total[w:])
            wst[f, 0, q] = hi
            wst[f, 1, q] = lo
            p_hi, p_lo = split(total[:w])
            lhs = jnp.concatenate([p_hi, p_lo], axis=0)
            for k in range(group):
                p = q * group + k
                b = block(f, p)
                both = dot(lhs, ctp[f, p])
                hi, lo = split(both[:w] + both[w:])
                hs[f, :, b * bs : (b + 1) * bs] = jnp.concatenate([hi, hi, lo, lo], axis=0)

    def pushes(f, piece):
        parts = []
        for q in range(quads):
            total = None
            for k in range(group):
                p = q * group + k
                v = piece(block(f, p))
                term = dot_nt(v, ntp[f, 0, p]) + dot_nt(v, ntp[f, 1, p])
                total = term if total is None else total + term
            parts.append(total)
        return jnp.concatenate(parts, axis=1)

    def message(f, u):
        return dot_split(u, wst[f, 0, quads], wst[f, 1, quads])

    def local_blocks(f, piece, u):
        out = {}
        for q in range(quads):
            x_hi, x_lo = split(dot_split(u, wst[f, 0, q], wst[f, 1, q]))
            lhs = jnp.concatenate([x_hi, x_lo], axis=0)
            for k in range(group):
                p = q * group + k
                b = block(f, p)
                both = dot(lhs, ctp[f, p])
                out[b] = dot_nt(piece(b), inv[f, b]) - both[:n] - both[n:]
        return out

    def cols(b):
        return slice(b * bs, (b + 1) * bs)

    def fold(m, z):
        mixed = jnp.where(lax.rem(lanes(n) // w, 2) == 0, m, z)
        return jnp.where(lanes(half) < LANES // 2, mixed[:half], mixed[half:])

    def unfold(x):
        low = lanes(half) < LANES // 2
        return jnp.concatenate([jnp.where(low, x, 0.0), jnp.where(low, 0.0, x)], axis=0)

    def copy(k, src, dst, i):
        peer = lax.rem(me + i + 1, R)
        return pltpu.make_async_remote_copy(
            src_ref=src, dst_ref=dst.at[me], send_sem=send_sem.at[k, i],
            recv_sem=recv_sem.at[k, me], device_id={"rows": peer}, device_id_type=MESH,
        )

    def arrive(k, src, dst, i):
        peer = lax.rem(me + i + 1, R)
        pltpu.make_async_remote_copy(
            src_ref=src, dst_ref=dst.at[peer], send_sem=send_sem.at[k, i],
            recv_sem=recv_sem.at[k, peer], device_id={"rows": peer}, device_id_type=MESH,
        ).wait_recv()

    def sweep_start(piece):
        u = pushes(0, piece)
        m = message(0, u)
        out = local_blocks(0, piece, u)
        for b in range(nb):
            y[:, cols(b)] = out[b]
        return m

    def incoming(arrived):
        a = jnp.concatenate([unfold(arrived(e)) for e in range(R)], axis=1)
        a_hi, a_lo = split(a)
        both = jnp.concatenate([a_hi, a_lo], axis=0)
        states = []
        for k in (0, 1):
            r = dot(both, table[k, 0])
            s_hi, s_lo = split(r[:n] + r[n:] + dot(a_hi, table[k, 1]))
            even = lax.rem(lanes(n) // w, 2) == 0
            states.append(jnp.where(even, s_hi.astype(f32), s_lo.astype(f32)).astype(bf16))
        return states

    def sweep_end(s_f, s_b, out_ref):
        forward = [
            (y[:, cols(b)] - dot(s_f, hs[0, :, cols(b)])).astype(bf16) for b in range(nb)
        ]
        piece = lambda b: forward[b]
        u = pushes(1, piece)
        out = local_blocks(1, piece, u)
        for b in range(nb):
            out_ref[:, cols(b)] = out[b] - dot(s_b, hs[1, :, cols(b)])

    m = sweep_start(lambda b: rhs[:, cols(b)])
    mixed = pushes(
        1,
        lambda b: jnp.concatenate(
            [*split(y[:, cols(b)]), hs[0, :w, cols(b)], hs[0, 2 * w : 3 * w, cols(b)]], axis=0
        ),
    )
    u = jnp.concatenate(
        [mixed[:n] + mixed[n : 2 * n], mixed[2 * n : 2 * n + w] + mixed[2 * n + w :]], axis=0
    )
    zm = message(1, u)
    send1[:w] = jnp.where(
        lane < w, maps[0], jnp.where(lane < 2 * w, maps[1], jnp.where(lane < 3 * w, zm[n:], 0.0))
    )
    send1[w:] = fold(m, zm[:n])
    pl.semaphore_wait(barrier, R - 1)
    each(R - 1, lambda i: copy(0, send1, got1, i).start())
    got1[me] = send1[...]
    each(R - 1, lambda i: arrive(0, send1, got1, i))

    def mapped(e, k, v):
        t = jnp.where(lane // w == k, got1[e, :w], 0.0)
        return dot_full(t, jnp.concatenate([v] * group, axis=0))

    zero = jnp.zeros((w, LANES), f32)
    g[0, R - 1] = zero
    g[1, 0] = zero
    g[2, R - 1] = zero

    def chains(i):
        d = i
        g[1, d + 1] = mapped(d, 1, g[1, d]) + jnp.where(me == d, eye, 0.0)
        d = R - 1 - i
        g[0, d - 1] = mapped(d, 0, g[0, d]) + jnp.where(me == d, eye, 0.0)

    each(R - 1, chains)

    def cross(i):
        d = R - 1 - i
        g[2, d - 1] = mapped(d, 0, g[2, d]) + mapped(d, 2, g[1, d])

    each(R - 1, cross)

    def fill(e):
        at = pl.ds(e * LANES if isinstance(e, int) else pl.multiple_of(e * LANES, LANES), LANES)
        hi, lo = split(jnp.concatenate([g[0, e], zero] * 2, axis=0))
        table[0, 0, at] = hi
        table[0, 1, at] = lo
        hi, lo = split(jnp.concatenate([-g[2, e], g[1, e]] * 2, axis=0))
        table[1, 0, at] = hi
        table[1, 1, at] = lo

    each(R, fill)

    s_f, s_b = incoming(lambda e: got1[e, w:])
    sweep_end(s_f, s_b, first)

    m = sweep_start(lambda b: first[:, cols(b)].astype(bf16))
    mixed = pushes(1, lambda b: jnp.concatenate(split(y[:, cols(b)]), axis=0))
    z = message(1, mixed[:n] + mixed[n:])
    send2[...] = fold(m, z)
    each(R - 1, lambda i: copy(1, send2, got2, i).start())
    got2[me] = send2[...]
    each(R - 1, lambda i: arrive(1, send2, got2, i))
    s_f, s_b = incoming(lambda e: got2[e])
    sweep_end(s_f, s_b, second)

    each(R - 1, lambda i: copy(0, send1, got1, i).wait_send())
    each(R - 1, lambda i: copy(1, send2, got2, i).wait_send())


def local(R, rhs, linv, lleft, lright, uinv, uleft, uright, ranks):
    nb, bs, w = lleft.shape
    n = rhs.shape[0]
    flip = lambda a: jnp.swapaxes(a, 1, 2)
    vmem = pl.BlockSpec(memory_space=pltpu.VMEM)
    hbm = pl.BlockSpec(memory_space=pl.ANY)
    smem = pl.BlockSpec(memory_space=pltpu.SMEM)
    quads = nb * w // LANES
    out = jax.ShapeDtypeStruct(rhs.shape, f32)
    packed = w + n // 2
    return pl.pallas_call(
        functools.partial(kernel, R, nb, bs, w, n),
        out_shape=(out, out),
        in_specs=[vmem, hbm, vmem, vmem, hbm, vmem, vmem, smem],
        out_specs=(vmem, vmem),
        scratch_shapes=[
            pltpu.VMEM((2, nb, bs, bs), bf16),
            pltpu.VMEM((2, nb, LANES, bs), bf16),
            pltpu.VMEM((2, 2, nb, LANES, bs), bf16),
            pltpu.VMEM((2, 2, quads + 1, nb * w, LANES), bf16),
            pltpu.VMEM((2, 4 * w, nb * bs), bf16),
            pltpu.VMEM((R, packed, LANES), f32),
            pltpu.VMEM((R, n // 2, LANES), f32),
            pltpu.VMEM((packed, LANES), f32),
            pltpu.VMEM((n // 2, LANES), f32),
            pltpu.VMEM((3, R, w, LANES), f32),
            pltpu.VMEM((2, 2, R * LANES, LANES), bf16),
            pltpu.VMEM((n, nb * bs), f32),
            pltpu.SemaphoreType.DMA((2,)),
            pltpu.SemaphoreType.DMA((2, R)),
            pltpu.SemaphoreType.DMA((2, R)),
        ],
        compiler_params=pltpu.CompilerParams(
            collective_id=0, has_side_effects=True, vmem_limit_bytes=48 * 1024 * 1024
        ),
    )(rhs, linv, flip(lleft), flip(lright), uinv, flip(uleft), flip(uright), ranks)


def solution(mesh):
    blocks = P("rows", None, None)
    placed = (P("rhs", "rows"),) + (blocks,) * 6 + (P(None, "rows"),)
    return jax.shard_map(
        functools.partial(local, mesh.shape["rows"]),
        mesh=mesh,
        in_specs=placed,
        out_specs=(P("rhs", "rows"), P("rhs", "rows")),
        check_vma=False,
    )
```

```python
import functools

import jax
import jax.numpy as jnp
from jax import lax
from jax.experimental import pallas as pl
from jax.experimental.pallas import tpu as pltpu
from jax.sharding import PartitionSpec as P

MESH = pl.DeviceIdType.MESH
LANES = 128
f32, bf16 = jnp.float32, jnp.bfloat16


def split(x):
    hi = x.astype(bf16)
    return hi, (x - hi.astype(f32)).astype(bf16)


def dot(a, b):
    return jnp.dot(a, b, preferred_element_type=f32)


def dot_nt(a, b):
    return lax.dot_general(a, b, (((1,), (1,)), ((), ())), preferred_element_type=f32)


def dot_split(a, b_hi, b_lo):
    a_hi, a_lo = split(a)
    rows = a.shape[0]
    both = dot(jnp.concatenate([a_hi, a_lo], axis=0), b_hi)
    return both[:rows] + both[rows:] + dot(a_hi, b_lo)


def dot_full(a, b):
    return dot_split(a, *split(b))


def grow(x, rows):
    if x.shape[0] == rows:
        return x
    return jnp.concatenate([x, jnp.zeros((rows - x.shape[0], LANES), f32)], axis=0)


def each(count, body):
    if count <= 8:
        for i in range(count):
            body(i)
    else:
        lax.fori_loop(0, count, lambda i, c: (body(i), c)[1], 0)


def kernel(
    R, nb, bs, w, n,
    rhs_h, linv_h, llt_h, lrt_h, uinv_h, ult_h, urt_h, ranks_h,
    first, second,
    rhs, llt, lrt, ult, urt, ranks,
    inv, ctp, ntp, wst, hs, got0, got1, got2, send0, send1, send2, g, walk, table, y,
    load_sem, block_sem, send_sem, recv_sem,
):
    me = lax.axis_index("rows")
    group = LANES // w
    quads = nb // group
    half = n // 2

    small = [
        pltpu.make_async_copy(src, dst, load_sem.at[i])
        for i, (src, dst) in enumerate(
            ((llt_h, llt), (lrt_h, lrt), (ranks_h, ranks), (ult_h, ult), (urt_h, urt), (rhs_h, rhs))
        )
    ]
    large = [
        [
            pltpu.make_async_copy(src.at[b], inv.at[f, b], block_sem.at[f, b])
            for b in (range(nb) if f == 0 else reversed(range(nb)))
        ]
        for f, src in ((0, linv_h), (1, uinv_h))
    ]
    for cp in small[:3] + large[0] + small[3:5] + large[1] + small[5:]:
        cp.start()

    barrier = pltpu.get_barrier_semaphore()

    def greet(i):
        pl.semaphore_signal(
            barrier, inc=1, device_id={"rows": lax.rem(me + i + 1, R)}, device_id_type=MESH
        )

    each(R - 1, greet)

    ctp[...] = jnp.zeros_like(ctp)
    ntp[...] = jnp.zeros_like(ntp)

    lane = lax.broadcasted_iota(jnp.int32, (w, LANES), 1)
    row = lax.broadcasted_iota(jnp.int32, (w, LANES), 0)
    eye = (lax.rem(lane, w) == row).astype(f32)

    def lanes(rows):
        return lax.broadcasted_iota(jnp.int32, (rows, LANES), 1)

    def block(f, p):
        return p if f == 0 else nb - 1 - p

    lefts, rights = (llt, ult), (lrt, urt)
    kernels = ([], [])
    maps = [None, None]
    for f in (0, 1):
        for cp in small[:3] if f == 0 else small[3:5]:
            cp.wait()
        wide_row = lax.broadcasted_iota(jnp.int32, (w, bs), 0)
        for p in range(nb):
            b = block(f, p)
            large[f][p].wait()
            at = pl.ds(w * (p % group), w)
            ct = dot_nt(lefts[f][b], inv[f, b]).astype(bf16)
            ctp[f, p, at, :] = ct
            mt = jnp.where(wide_row < ranks[f, b], rights[f][b].astype(f32), 0.0).astype(bf16)
            hi, lo = split(dot(mt, inv[f, b]))
            ntp[f, 0, p, at, :] = hi
            ntp[f, 1, p, at, :] = lo
            kernels[f].append(eye - dot_nt(ct, jnp.concatenate([mt] * group, axis=0)))

    chains = {}
    for q in range(quads):
        for f in (0, 1):
            chains[f, q] = [eye]
    for k in range(group):
        for q in range(quads):
            for f in (0, 1):
                last = chains[f, q][-1]
                moved = dot_full(last[:, :w], kernels[f][q * group + k])
                chains[f, q].append(jnp.concatenate([moved, eye], axis=0))

    full = w * (nb + 1)
    joined = {}
    for f in (0, 1):
        before = None
        for q in range(quads):
            grown = w * (group + 1)
            total = jnp.zeros((grown, LANES), f32)
            for k in range(group):
                col = chains[f, q][k]
                total = jnp.where(lanes(grown) // w == k, grow(col, grown), total)
            end = chains[f, q][group]
            if before is not None:
                moved = dot_full(before[:, :w], jnp.concatenate([total[:w], end[:w]], axis=1))
                total = jnp.concatenate([moved[:, :LANES], total[w:]], axis=0)
                end = jnp.concatenate([moved[:, LANES:], end[w:]], axis=0)
            joined[f, q] = grow(total, full)
            before = end
        maps[f] = before[:w]
        hi, lo = split(before[w:])
        wst[f, 0, quads] = hi
        wst[f, 1, quads] = lo

    narrow = w // group
    narrow_lanes = lanes(narrow) // w

    def fold_map(x):
        out = x[:narrow]
        for k in range(1, group):
            out = jnp.where(narrow_lanes == k, x[k * narrow : (k + 1) * narrow], out)
        return out

    def tile(x):
        return jnp.concatenate([x] * group, axis=0)

    def expand(x):
        return jnp.where(lane // w == row // narrow, tile(x), 0.0)

    def copy(k, src, dst, i):
        peer = lax.rem(me + i + 1, R)
        return pltpu.make_async_remote_copy(
            src_ref=src, dst_ref=dst.at[me], send_sem=send_sem.at[k, i],
            recv_sem=recv_sem.at[k, me], device_id={"rows": peer}, device_id_type=MESH,
        )

    def arrive(k, src, dst, i):
        peer = lax.rem(me + i + 1, R)
        pltpu.make_async_remote_copy(
            src_ref=src, dst_ref=dst.at[peer], send_sem=send_sem.at[k, i],
            recv_sem=recv_sem.at[k, peer], device_id={"rows": peer}, device_id_type=MESH,
        ).wait_recv()

    send0[:narrow] = fold_map(maps[0])
    send0[narrow:] = fold_map(maps[1])
    pl.semaphore_wait(barrier, R - 1)
    each(R - 1, lambda i: copy(0, send0, got0, i).start())
    got0[me] = send0[...]

    for f in (0, 1):
        for q in range(quads):
            total = joined[f, q]
            hi, lo = split(total[w:])
            wst[f, 0, q] = hi
            wst[f, 1, q] = lo
            p_hi, p_lo = split(total[:w])
            lhs = jnp.concatenate([p_hi, p_lo], axis=0)
            for k in range(group):
                p = q * group + k
                b = block(f, p)
                both = dot(lhs, ctp[f, p])
                hi, lo = split(both[:w] + both[w:])
                hs[f, :, b * bs : (b + 1) * bs] = jnp.concatenate([hi, hi, lo, lo], axis=0)

    def pushes(f, piece):
        parts = []
        for q in range(quads):
            total = None
            for k in range(group):
                p = q * group + k
                v = piece(block(f, p))
                term = dot_nt(v, ntp[f, 0, p]) + dot_nt(v, ntp[f, 1, p])
                total = term if total is None else total + term
            parts.append(total)
        return jnp.concatenate(parts, axis=1)

    def message(f, u):
        return dot_split(u, wst[f, 0, quads], wst[f, 1, quads])

    def local_blocks(f, piece, u):
        out = {}
        for q in range(quads):
            x_hi, x_lo = split(dot_split(u, wst[f, 0, q], wst[f, 1, q]))
            lhs = jnp.concatenate([x_hi, x_lo], axis=0)
            for k in range(group):
                p = q * group + k
                b = block(f, p)
                both = dot(lhs, ctp[f, p])
                out[b] = dot_nt(piece(b), inv[f, b]) - both[:n] - both[n:]
        return out

    def cols(b):
        return slice(b * bs, (b + 1) * bs)

    def fold(m, z):
        mixed = jnp.where(lax.rem(lanes(n) // w, 2) == 0, m, z)
        return jnp.where(lanes(half) < LANES // 2, mixed[:half], mixed[half:])

    def unfold(x):
        low = lanes(half) < LANES // 2
        return jnp.concatenate([jnp.where(low, x, 0.0), jnp.where(low, 0.0, x)], axis=0)

    def sweep_start(piece):
        u = pushes(0, piece)
        m = message(0, u)
        out = local_blocks(0, piece, u)
        for b in range(nb):
            y[:, cols(b)] = out[b]
        return m

    def incoming(arrived):
        a = jnp.concatenate([unfold(arrived(e)) for e in range(R)], axis=1)
        a_hi, a_lo = split(a)
        both = jnp.concatenate([a_hi, a_lo], axis=0)
        states = []
        for k in (0, 1):
            r = dot(both, table[k, 0])
            s_hi, s_lo = split(r[:n] + r[n:] + dot(a_hi, table[k, 1]))
            even = lax.rem(lanes(n) // w, 2) == 0
            states.append(jnp.where(even, s_hi.astype(f32), s_lo.astype(f32)).astype(bf16))
        return states

    def sweep_end(s_f, s_b, out_ref):
        forward = [
            (y[:, cols(b)] - dot(s_f, hs[0, :, cols(b)])).astype(bf16) for b in range(nb)
        ]
        piece = lambda b: forward[b]
        u = pushes(1, piece)
        out = local_blocks(1, piece, u)
        for b in range(nb):
            out_ref[:, cols(b)] = out[b] - dot(s_b, hs[1, :, cols(b)])

    small[5].wait()
    m = sweep_start(lambda b: rhs[:, cols(b)])
    mixed = pushes(
        1,
        lambda b: jnp.concatenate(
            [*split(y[:, cols(b)]), hs[0, :w, cols(b)], hs[0, 2 * w : 3 * w, cols(b)]], axis=0
        ),
    )
    u = jnp.concatenate(
        [mixed[:n] + mixed[n : 2 * n], mixed[2 * n : 2 * n + w] + mixed[2 * n + w :]], axis=0
    )
    zm = message(1, u)
    send1[:narrow] = fold_map(zm[n:])
    send1[narrow:] = fold(m, zm[:n])
    each(R - 1, lambda i: copy(1, send1, got1, i).start())
    got1[me] = send1[...]

    zero = jnp.zeros((w, LANES), f32)
    spot = jnp.where(lane < w, eye, 0.0)
    each(R - 1, lambda i: arrive(0, send0, got0, i))
    g[1, 0:w] = zero

    def rows_of(d):
        return pl.ds(d * w if isinstance(d, int) else pl.multiple_of(d * w, w), w)

    def backward_map(d):
        moved = dot_full(expand(got0[d, narrow:]), tile(g[1, rows_of(d)]))
        g[1, rows_of(d + 1)] = moved + jnp.where(me == d, eye, 0.0)

    def forward_map(d, state):
        return dot_full(state, tile(expand(got0[d, :narrow])))

    def crossed(d, state):
        return dot_full(
            dot_full(state, tile(expand(got1[d, :narrow]))), tile(g[1, rows_of(d)])
        )

    if R <= 8:
        history = [None]
        for d in range(R - 1):
            backward_map(d)
            last = history[-1]
            grown = spot if last is None else jnp.concatenate([forward_map(d, last), spot], axis=0)
            history.append(grown)
        chosen = jnp.zeros((R * w, LANES), f32)
        for d in range(1, R):
            chosen = jnp.where(me == d, grow(history[d], R * w), chosen)
        g[0] = chosen
        each(R - 1, lambda i: arrive(1, send1, got1, i))
        total = jnp.zeros((R * w, LANES), f32)
        for d in range(1, R):
            total += grow(crossed(d, history[d]), R * w)
        g[2] = total
    else:
        each(R - 1, backward_map)
        each(R - 1, lambda i: arrive(1, send1, got1, i))
        walk[...] = jnp.zeros_like(walk)
        g[0] = jnp.zeros((R * w, LANES), f32)
        g[2] = jnp.zeros((R * w, LANES), f32)

        def step(d):
            state = walk[...]
            g[0] = jnp.where(me == d, state, g[0])
            g[2] = g[2] + crossed(d, state)
            walk[...] = forward_map(d, state)
            walk[rows_of(d)] = spot

        each(R, step)

    c_hi, c_lo = split(g[0])
    spread = tile(eye).astype(bf16)
    g[0] = dot(c_hi, spread) + dot(c_lo, spread)

    def fill(e):
        at = pl.ds(e * LANES if isinstance(e, int) else pl.multiple_of(e * LANES, LANES), LANES)
        hi, lo = split(jnp.concatenate([g[0, rows_of(e)], zero] * 2, axis=0))
        table[0, 0, at] = hi
        table[0, 1, at] = lo
        hi, lo = split(jnp.concatenate([-g[2, rows_of(e)], g[1, rows_of(e)]] * 2, axis=0))
        table[1, 0, at] = hi
        table[1, 1, at] = lo

    each(R, fill)

    s_f, s_b = incoming(lambda e: got1[e, narrow:])
    sweep_end(s_f, s_b, first)

    m = sweep_start(lambda b: first[:, cols(b)].astype(bf16))
    mixed = pushes(1, lambda b: jnp.concatenate(split(y[:, cols(b)]), axis=0))
    z = message(1, mixed[:n] + mixed[n:])
    send2[...] = fold(m, z)
    each(R - 1, lambda i: copy(2, send2, got2, i).start())
    got2[me] = send2[...]
    each(R - 1, lambda i: arrive(2, send2, got2, i))
    s_f, s_b = incoming(lambda e: got2[e])
    sweep_end(s_f, s_b, second)

    each(R - 1, lambda i: copy(0, send0, got0, i).wait_send())
    each(R - 1, lambda i: copy(1, send1, got1, i).wait_send())
    each(R - 1, lambda i: copy(2, send2, got2, i).wait_send())


def local(R, rhs, linv, lleft, lright, uinv, uleft, uright, ranks):
    nb, bs, w = lleft.shape
    n = rhs.shape[0]
    flip = lambda a: jnp.swapaxes(a, 1, 2)
    vmem = pl.BlockSpec(memory_space=pltpu.VMEM)
    hbm = pl.BlockSpec(memory_space=pltpu.HBM)
    quads = nb * w // LANES
    out = jax.ShapeDtypeStruct(rhs.shape, f32)
    narrow = w * w // LANES
    packed = narrow + n // 2
    slim = pltpu.VMEM((nb, w, bs), bf16)
    return pl.pallas_call(
        functools.partial(kernel, R, nb, bs, w, n),
        out_shape=(out, out),
        in_specs=[hbm] * 8,
        out_specs=(vmem, vmem),
        scratch_shapes=[
            pltpu.VMEM(rhs.shape, bf16),
            slim, slim, slim, slim,
            pltpu.SMEM(ranks.shape, jnp.int32),
            pltpu.VMEM((2, nb, bs, bs), bf16),
            pltpu.VMEM((2, nb, LANES, bs), bf16),
            pltpu.VMEM((2, 2, nb, LANES, bs), bf16),
            pltpu.VMEM((2, 2, quads + 1, nb * w, LANES), bf16),
            pltpu.VMEM((2, 4 * w, nb * bs), bf16),
            pltpu.VMEM((R, 2 * narrow, LANES), f32),
            pltpu.VMEM((R, packed, LANES), f32),
            pltpu.VMEM((R, n // 2, LANES), f32),
            pltpu.VMEM((2 * narrow, LANES), f32),
            pltpu.VMEM((packed, LANES), f32),
            pltpu.VMEM((n // 2, LANES), f32),
            pltpu.VMEM((3, R * w, LANES), f32),
            pltpu.VMEM((R * w, LANES), f32),
            pltpu.VMEM((2, 2, R * LANES, LANES), bf16),
            pltpu.VMEM((n, nb * bs), f32),
            pltpu.SemaphoreType.DMA((6,)),
            pltpu.SemaphoreType.DMA((2, nb)),
            pltpu.SemaphoreType.DMA((3, R)),
            pltpu.SemaphoreType.DMA((3, R)),
        ],
        compiler_params=pltpu.CompilerParams(
            collective_id=0, has_side_effects=True, vmem_limit_bytes=67043328
        ),
    )(rhs, linv, flip(lleft), flip(lright), uinv, flip(uleft), flip(uright), ranks)


def solution(mesh):
    blocks = P("rows", None, None)
    placed = (P("rhs", "rows"),) + (blocks,) * 6 + (P(None, "rows"),)
    return jax.shard_map(
        functools.partial(local, mesh.shape["rows"]),
        mesh=mesh,
        in_specs=placed,
        out_specs=(P("rhs", "rows"), P("rhs", "rows")),
        check_vma=False,
    )
```
